32 devices in a mesh: gx: 2 (over y), gy: 4 (over x, core), gz: 4 (over z).
Axes of the slice: x: 2, y: 2, z: 4, core: 2. Of those that a mesh axis runs over, the one named last changes fastest.
Arguments:
- wavefunctions: bfloat16 [32, 64, 64, 128], P('gx', 'gy', 'gz'), may hold values from -512 to 512, as said below
- potential: float32 [32, 64, 64], P('gx', 'gy', 'gz'), may hold values from 0 to 3
Outputs:
- rotated: float32 [32, 64, 64, 128], P('gx', 'gy', 'gz')
- residual: bfloat16 [32, 64, 64, 128], P('gx', 'gy', 'gz')
- quotients: float32 [128], replicated
- norms: float32 [128], replicated
The draws below stay inside these ranges and needn't reach their ends.
Inputs may be any that keep to these rules, and one draw needn't show every extreme that they name: `wavefunctions`: real values mixed across bands, of full rank.
All inputs are finite; a program needn't handle non-finite values.
Results may differ from the reference program's by a relative error of at most 0.0007.
Values may be sent and summed in bfloat16 or wider, within the bound.
A program may use at most 64 MiB of HBM per device.

```python
import jax
import jax.numpy as jnp
from jax import lax

BANDS = 128
NX = 32
NY = 64
NZ = 64


def draw_wavefunctions(key, part):
    first, second, third = jax.random.split(jax.random.fold_in(key, 17), 3)
    values = jnp.clip(jax.random.normal(first, (NX, NY, NZ, BANDS), jnp.float32), -4.0, 4.0)
    scales = jnp.exp(jax.random.uniform(third, (BANDS,), jnp.float32, jnp.log(0.3), jnp.log(3.0)))
    mixing = jnp.eye(BANDS, dtype=jnp.float32) + 0.4 * jnp.clip(jax.random.normal(second, (BANDS, BANDS), jnp.float32), -3.0, 3.0) / jnp.sqrt(BANDS * 1.0)
    mixed = jnp.einsum('xyzb,bc->xyzc', values, mixing) * scales
    along_x = jnp.arange(NX, dtype=jnp.float32) / NX
    along_y = jnp.arange(NY, dtype=jnp.float32) / NY
    along_z = jnp.arange(NZ, dtype=jnp.float32) / NZ
    envelope = 0.5 * jnp.exp(0.55 * (along_x[:, None, None] + along_y[None, :, None] + along_z[None, None, :]))
    return (mixed * envelope[..., None]).astype(jnp.bfloat16)


def level_of(key, extent, cuts, smallest, high):
    factor_of, own = 1.0, jax.random.fold_in(key, 6)
    for axis_at, parts in cuts:
        steps = jnp.exp(jax.random.uniform(jax.random.fold_in(own, axis_at), (parts,), jnp.float32, smallest / len(cuts), high / len(cuts)))
        factor_of = factor_of * jnp.repeat(steps, extent[axis_at] // parts).reshape([-1 if axis == axis_at else 1 for axis in range(len(extent))])
    return factor_of


def setup_inputs(seed: int = 0) -> dict:
    key_list = jax.random.split(jax.random.key(seed), 3)
    wavefunctions = draw_wavefunctions(jax.random.fold_in(key_list[2], 71), 0)
    potential = jnp.clip(3.0 * jax.random.uniform(key_list[1], (NX, NY, NZ), jnp.float32) ** level_of(key_list[1], (NX, NY, NZ), ((0, 2), (1, 4), (2, 4)), -0.2, 0.2), 0.0, 3.0)
    return {"wavefunctions": wavefunctions, "potential": potential}


def kinetic(field):
    total = jnp.zeros_like(field)
    for axis in range(3):
        total = total + (-jnp.roll(field, 2, axis) + 16.0 * jnp.roll(field, 1, axis) - 30.0 * field + 16.0 * jnp.roll(field, -1, axis) - jnp.roll(field, -2, axis)) / 12.0
    return -0.5 * total

def reference(wavefunctions, potential):
    cells = NX * NY * NZ
    flat = wavefunctions.reshape(cells, BANDS)
    correlation = lax.dot_general(flat.astype(jnp.float32), flat.astype(jnp.float32), (((0,), (0,)), ((), ())), preferred_element_type=jnp.float32) / cells
    factor = jnp.linalg.cholesky(correlation)
    inverse = lax.linalg.triangular_solve(factor, jnp.eye(BANDS, dtype=jnp.float32), left_side=True, lower=True)
    rotated = jnp.dot(flat.astype(jnp.float32), inverse.T, precision=lax.Precision.HIGHEST).reshape(NX, NY, NZ, BANDS)
    width = BANDS // 8
    pieces, quotient_list, norm_list = ([], [], [])
    for block in range(8):
        part = rotated[..., block * width:(block + 1) * width]
        applied = kinetic(part) + potential[..., None] * part
        quotient = lax.optimization_barrier(jnp.sum(part * applied, axis=(0, 1, 2))) / cells
        leftover = applied - quotient * part
        norm_value = jnp.sqrt(lax.optimization_barrier(jnp.sum(leftover * leftover, axis=(0, 1, 2))) / cells + 1e-06)
        pieces.append(leftover.astype(jnp.bfloat16))
        quotient_list.append(quotient)
        norm_list.append(norm_value)
    residual = jnp.concatenate(pieces, axis=3)
    return (rotated, residual, jnp.concatenate(quotient_list), jnp.concatenate(norm_list))
```

```python
import functools

import jax
import jax.numpy as jnp
from jax import lax
from jax.experimental import pallas as pl
from jax.experimental.pallas import tpu as pltpu
from jax.sharding import PartitionSpec as P

MESH = pl.DeviceIdType.MESH
F32 = jnp.float32
BF16 = jnp.bfloat16


def split2(a):
    hi = a.astype(BF16)
    return hi, (a - hi.astype(F32)).astype(BF16)


def split3(a):
    hi = a.astype(BF16)
    rest = a - hi.astype(F32)
    mid = rest.astype(BF16)
    return hi, mid, (rest - mid.astype(F32)).astype(BF16)


def gram(a, b):
    return lax.dot_general(a, b, (((0,), (0,)), ((), ())), preferred_element_type=F32)


def reduce_kernel(sizes, p_any, v_ref, hi_ref, lo_ref, sum_ref,
                  pext, ylo, yhi, zlo, zhi, zsend, part, got1, acc, got2, total, gathered,
                  load_sem, hs, hr, s1, r1, s2, r2, s3, r3):
    nx, ny, nz = sizes
    ne = nx * nz
    cx, cy, cz, bands = p_any.shape
    mx, my, mz = lax.axis_index("gx"), lax.axis_index("gy"), lax.axis_index("gz")
    me = mx * nz + mz

    def line_peer(offset):
        return (mx, lax.rem(my + offset, ny), mz)

    def plane_peer(offset):
        e = lax.rem(me + offset, ne)
        return (e // nz, my, lax.rem(e, nz))

    load = pltpu.make_async_copy(p_any, pext.at[pl.ds(2, cx)], load_sem)
    load.start()
    barrier = pltpu.get_barrier_semaphore()
    for o in range(1, ny):
        pl.semaphore_signal(barrier, inc=1, device_id=line_peer(o), device_id_type=MESH)
    for o in range(1, ne):
        pl.semaphore_signal(barrier, inc=1, device_id=plane_peer(o), device_id_type=MESH)
    load.wait()
    own = pext[2:2 + cx]
    zsend[0] = own[:, :, cz - 2:, :]
    zsend[1] = own[:, :, :2, :]
    pl.semaphore_wait(barrier, ny - 1 + ne - 1)

    def remote(src, dst, i, device):
        return pltpu.make_async_remote_copy(src_ref=src, dst_ref=dst, send_sem=hs.at[i], recv_sem=hr.at[i],
                                            device_id=device, device_id_type=MESH)

    xf = (lax.rem(mx + 1, nx), my, mz)
    xb = (lax.rem(mx + nx - 1, nx), my, mz)
    yf = (mx, lax.rem(my + 1, ny), mz)
    yb = (mx, lax.rem(my + ny - 1, ny), mz)
    zf = (mx, my, lax.rem(mz + 1, nz))
    zb = (mx, my, lax.rem(mz + nz - 1, nz))
    halos = [
        remote(zsend.at[0], zlo, 0, zf),
        remote(zsend.at[1], zhi, 1, zb),
        remote(p_any.at[pl.ds(cx - 2, 2)], pext.at[pl.ds(0, 2)], 2, xf),
        remote(p_any.at[pl.ds(0, 2)], pext.at[pl.ds(cx + 2, 2)], 3, xb),
        remote(p_any.at[:, pl.ds(cy - 2, 2)], ylo, 4, yf),
        remote(p_any.at[:, pl.ds(0, 2)], yhi, 5, yb),
    ]
    for copy in halos:
        copy.start()
    flat = pext[2:2 + cx].reshape(cx * cy * cz, bands)
    rows = bands // ny

    def put(slot, matrix):
        for k in range(ny):
            part[k, slot * rows:(slot + 1) * rows] = matrix[k * rows:(k + 1) * rows]

    put(0, gram(flat, flat))
    for copy in halos:
        copy.wait()

    def plane(i, carry):
        center = pext[i + 2].astype(F32)
        one, two = 16.0 / -24.0, 1.0 / 24.0
        near = pext[i + 1].astype(F32) + pext[i + 3].astype(F32)
        far = pext[i].astype(F32) + pext[i + 4].astype(F32)
        ye = jnp.concatenate([ylo[i].astype(F32), center, yhi[i].astype(F32)], axis=0)
        near = near + (ye[1:1 + cy] + ye[3:3 + cy])
        far = far + (ye[0:cy] + ye[4:4 + cy])
        ze = jnp.concatenate([zlo[i].astype(F32), center, zhi[i].astype(F32)], axis=1)
        near = near + (ze[:, 1:1 + cz] + ze[:, 3:3 + cz])
        far = far + (ze[:, 0:cz] + ze[:, 4:4 + cz])
        level = v_ref[i][:, :, None] + 90.0 / 24.0
        applied = one * near + two * far + level * center
        hi, lo = split2(applied)
        hi_ref[i] = hi
        lo_ref[i] = lo
        return carry

    lax.fori_loop(0, cx, plane, 0)
    hi = hi_ref[...].reshape(cx * cy * cz, bands)
    lo = lo_ref[...].reshape(cx * cy * cz, bands)
    put(1, gram(flat, hi) + gram(flat, lo))
    cross = gram(hi, lo)
    put(2, gram(hi, hi) + cross + cross.T)

    copies = []
    for o in range(1, ny):
        copies.append(pltpu.make_async_remote_copy(
            src_ref=part.at[lax.rem(my + o, ny)], dst_ref=got1.at[o - 1], send_sem=s1.at[o - 1], recv_sem=r1.at[o - 1],
            device_id=line_peer(o), device_id_type=MESH))
        copies[-1].start()
    for copy in copies:
        copy.wait()
    mine = part[my]
    for o in range(1, ny):
        mine = mine + got1[o - 1]
    acc[...] = mine
    copies = []
    for o in range(1, ne):
        copies.append(pltpu.make_async_remote_copy(
            src_ref=acc, dst_ref=got2.at[me], send_sem=s2.at[o - 1], recv_sem=r2.at[o - 1],
            device_id=plane_peer(o), device_id_type=MESH))
        copies[-1].start()
    got2[me] = mine
    for o in range(1, ne):
        copies[o - 1].wait_send()
        pltpu.make_async_remote_copy(
            src_ref=acc, dst_ref=got2.at[lax.rem(me + ne - o, ne)], send_sem=s2.at[o - 1], recv_sem=r2.at[o - 1],
            device_id=plane_peer(o), device_id_type=MESH).wait_recv()
    whole = got2[0]
    for e in range(1, ne):
        whole = whole + got2[e]
    total[...] = whole
    copies = []
    for o in range(1, ny):
        copies.append(pltpu.make_async_remote_copy(
            src_ref=total, dst_ref=gathered.at[my], send_sem=s3.at[o - 1], recv_sem=r3.at[o - 1],
            device_id=line_peer(o), device_id_type=MESH))
        copies[-1].start()
    gathered[my] = whole
    for o in range(1, ny):
        copies[o - 1].wait_send()
        pltpu.make_async_remote_copy(
            src_ref=total, dst_ref=gathered.at[lax.rem(my + ny - o, ny)], send_sem=s3.at[o - 1], recv_sem=r3.at[o - 1],
            device_id=line_peer(o), device_id_type=MESH).wait_recv()
    for k in range(ny):
        for slot in range(3):
            sum_ref[slot, k * rows:(k + 1) * rows] = gathered[k, slot * rows:(slot + 1) * rows]


def invert(matrix):
    n = matrix.shape[0]
    lane = lax.broadcasted_iota(jnp.int32, (1, n), 1)
    lanes8 = lax.broadcasted_iota(jnp.int32, (8, n), 1)
    sub8 = lax.broadcasted_iota(jnp.int32, (8, n), 0)
    tiles = [matrix[8 * t:8 * t + 8] for t in range(n // 8)]
    for j in range(n - 1):
        t0, r = divmod(j, 8)
        row = tiles[t0][r:r + 1]
        scale = 1.0 / row[:, j:j + 1]
        row = jnp.where(lane == j, 1.0, row) * scale
        here = lanes8 == j
        for t in range(t0 if r < 7 else t0 + 1, n // 8):
            column = tiles[t][:, j:j + 1]
            new = jnp.where(here, 0.0, tiles[t]) - column * row
            tiles[t] = jnp.where(sub8 > r, new, tiles[t]) if t == t0 else new
    out = []
    for t in range(n // 8):
        diagonal = lanes8 == sub8 + 8 * t
        pivot = jnp.sum(jnp.where(diagonal, tiles[t], 0.0), axis=1, keepdims=True)
        unit = jnp.where(diagonal, 1.0, jnp.where(lanes8 < sub8 + 8 * t, tiles[t], 0.0))
        out.append(unit * lax.rsqrt(pivot))
    return jnp.concatenate(out, axis=0)


def dot(a, b):
    return jnp.dot(a, b, preferred_element_type=F32)


def finish_kernel(cells, sums_ref, p_ref, hi_ref, lo_ref, rot_ref, res_ref, quo_ref, norm_ref, split):
    bands = p_ref.shape[1]

    @pl.when(pl.program_id(0) == 0)
    def _():
        correlation = sums_ref[0] / cells
        inverse_t = invert(correlation).T
        for i, piece in enumerate(split3(inverse_t)):
            split[:, i * bands:(i + 1) * bands] = piece

        def quadratic(m):
            prod = jnp.dot(m, inverse_t, precision=lax.Precision.HIGHEST, preferred_element_type=F32)
            return jnp.sum(inverse_t * prod, axis=0, keepdims=True)

        rotated_all = quadratic(sums_ref[0])
        cross_all = quadratic(sums_ref[1])
        applied_all = quadratic(sums_ref[2])
        quotients = cross_all / cells
        squares = applied_all - 2.0 * quotients * cross_all + quotients * quotients * rotated_all
        quo_ref[...] = quotients
        norm_ref[...] = jnp.sqrt(squares / cells + 1e-06)

    p = p_ref[...]
    wide = dot(p, split[:, :2 * bands])
    rotated = wide[:, :bands] + (wide[:, bands:] + dot(p, split[:, 2 * bands:]))
    rot_ref[...] = rotated
    wide = dot(hi_ref[...], split[:, :2 * bands])
    applied = wide[:, :bands] + (wide[:, bands:] + dot(lo_ref[...], split[:, :bands]))
    res_ref[...] = (applied - quo_ref[...] * rotated).astype(BF16)


def local(sizes, wavefunctions, potential):
    nx, ny, nz = sizes
    ne = nx * nz
    cx, cy, cz, bands = wavefunctions.shape
    mine = cx * cy * cz
    rows = 3 * bands // ny
    vmem = pl.BlockSpec(memory_space=pltpu.VMEM)
    dma = pltpu.SemaphoreType.DMA
    hi, lo, sums = pl.pallas_call(
        functools.partial(reduce_kernel, sizes),
        out_shape=(
            jax.ShapeDtypeStruct(wavefunctions.shape, BF16),
            jax.ShapeDtypeStruct(wavefunctions.shape, BF16),
            jax.ShapeDtypeStruct((3, bands, bands), F32),
        ),
        in_specs=[pl.BlockSpec(memory_space=pl.ANY), vmem],
        out_specs=(vmem, vmem, vmem),
        scratch_shapes=[
            pltpu.VMEM((cx + 4, cy, cz, bands), BF16),
            pltpu.VMEM((cx, 2, cz, bands), BF16),
            pltpu.VMEM((cx, 2, cz, bands), BF16),
            pltpu.VMEM((cx, cy, 2, bands), BF16),
            pltpu.VMEM((cx, cy, 2, bands), BF16),
            pltpu.VMEM((2, cx, cy, 2, bands), BF16),
            pltpu.VMEM((ny, rows, bands), F32),
            pltpu.VMEM((ny - 1, rows, bands), F32),
            pltpu.VMEM((rows, bands), F32),
            pltpu.VMEM((ne, rows, bands), F32),
            pltpu.VMEM((rows, bands), F32),
            pltpu.VMEM((ny, rows, bands), F32),
            dma, dma((6,)), dma((6,)),
            dma((ny - 1,)), dma((ny - 1,)), dma((ne - 1,)), dma((ne - 1,)), dma((ny - 1,)), dma((ny - 1,)),
        ],
        compiler_params=pltpu.CompilerParams(collective_id=0, has_side_effects=True, vmem_limit_bytes=48 * 1024 * 1024),
    )(wavefunctions, potential)
    steps = 8 if mine % 128 == 0 else 1
    tile = mine // steps
    block = pl.BlockSpec((tile, bands), lambda i: (i, 0))
    line = pl.BlockSpec((1, bands), lambda i: (0, 0))
    rotated, residual, quotients, norms = pl.pallas_call(
        functools.partial(finish_kernel, float(mine * nx * ny * nz)),
        grid=(steps,),
        out_shape=(
            jax.ShapeDtypeStruct((mine, bands), F32),
            jax.ShapeDtypeStruct((mine, bands), BF16),
            jax.ShapeDtypeStruct((1, bands), F32),
            jax.ShapeDtypeStruct((1, bands), F32),
        ),
        in_specs=[pl.BlockSpec((3, bands, bands), lambda i: (0, 0, 0)), block, block, block],
        out_specs=(block, block, line, line),
        scratch_shapes=[pltpu.VMEM((bands, 3 * bands), BF16)],
        compiler_params=pltpu.CompilerParams(vmem_limit_bytes=48 * 1024 * 1024),
    )(sums, wavefunctions.reshape(mine, bands), hi.reshape(mine, bands), lo.reshape(mine, bands))
    shape = wavefunctions.shape
    return rotated.reshape(shape), residual.reshape(shape), quotients.reshape(bands), norms.reshape(bands)


def solution(mesh):
    sizes = (mesh.shape["gx"], mesh.shape["gy"], mesh.shape["gz"])
    placed = (P("gx", "gy", "gz", None), P("gx", "gy", "gz"))
    return jax.shard_map(
        functools.partial(local, sizes),
        mesh=mesh,
        in_specs=placed,
        out_specs=(P("gx", "gy", "gz", None), P("gx", "gy", "gz", None), P(), P()),
        check_vma=False,
    )
```

```python
import functools

import jax
import jax.numpy as jnp
from jax import lax
from jax.experimental import pallas as pl
from jax.experimental.pallas import tpu as pltpu
from jax.sharding import PartitionSpec as P

MESH = pl.DeviceIdType.MESH
F32 = jnp.float32
BF16 = jnp.bfloat16


def split2(a):
    hi = a.astype(BF16)
    return hi, (a - hi.astype(F32)).astype(BF16)


def split3(a):
    hi = a.astype(BF16)
    rest = a - hi.astype(F32)
    mid = rest.astype(BF16)
    return hi, mid, (rest - mid.astype(F32)).astype(BF16)


def gram(a, b):
    return lax.dot_general(a, b, (((0,), (0,)), ((), ())), preferred_element_type=F32)


class Reduce:
    def __init__(self, sizes, refs):
        self.part, self.got1, self.acc, self.got2, self.total, self.gathered = refs[:6]
        self.s1, self.r1, self.s2, self.r2, self.s3, self.r3 = refs[6:]
        self.nx, self.ny, self.nz = sizes
        self.ne = self.nx * self.nz
        self.mx, self.my, self.mz = lax.axis_index("gx"), lax.axis_index("gy"), lax.axis_index("gz")
        self.me = self.mx * self.nz + self.mz

    def line_peer(self, offset):
        return (self.mx, lax.rem(self.my + offset, self.ny), self.mz)

    def plane_peer(self, offset):
        e = lax.rem(self.me + offset, self.ne)
        return (e // self.nz, self.my, lax.rem(e, self.nz))

    def scatter_copy(self, o):
        return pltpu.make_async_remote_copy(
            src_ref=self.part.at[lax.rem(self.my + o, self.ny)], dst_ref=self.got1.at[o - 1],
            send_sem=self.s1.at[o - 1], recv_sem=self.r1.at[o - 1],
            device_id=self.line_peer(o), device_id_type=MESH)

    def exchange_copy(self, o, slot):
        return pltpu.make_async_remote_copy(
            src_ref=self.acc, dst_ref=self.got2.at[slot], send_sem=self.s2.at[o - 1], recv_sem=self.r2.at[o - 1],
            device_id=self.plane_peer(o), device_id_type=MESH)

    def gather_copy(self, o, slot):
        return pltpu.make_async_remote_copy(
            src_ref=self.total, dst_ref=self.gathered.at[slot], send_sem=self.s3.at[o - 1], recv_sem=self.r3.at[o - 1],
            device_id=self.line_peer(o), device_id_type=MESH)

    def scatter(self):
        for o in range(1, self.ny):
            self.scatter_copy(o).start()

    def exchange(self):
        for o in range(1, self.ny):
            self.scatter_copy(o).wait()
        mine = self.part[self.my]
        for o in range(1, self.ny):
            mine = mine + self.got1[o - 1]
        self.acc[...] = mine
        for o in range(1, self.ne):
            self.exchange_copy(o, self.me).start()
        self.got2[self.me] = mine

    def gather(self):
        for o in range(1, self.ne):
            self.exchange_copy(o, self.me).wait_send()
            self.exchange_copy(o, lax.rem(self.me + self.ne - o, self.ne)).wait_recv()
        whole = self.got2[0]
        for e in range(1, self.ne):
            whole = whole + self.got2[e]
        self.total[...] = whole
        for o in range(1, self.ny):
            self.gather_copy(o, self.my).start()
        self.gathered[self.my] = whole

    def finish(self):
        for o in range(1, self.ny):
            self.gather_copy(o, self.my).wait_send()
            self.gather_copy(o, lax.rem(self.my + self.ny - o, self.ny)).wait_recv()


def reduce_scratch(sizes, rows, bands):
    nx, ny, nz = sizes
    ne = nx * nz
    dma = pltpu.SemaphoreType.DMA
    chunk = rows // ny
    shapes = ((ny, chunk), (ny - 1, chunk), (chunk,), (ne, chunk), (chunk,), (ny, chunk))
    return [pltpu.VMEM(shape + (bands,), F32) for shape in shapes] + [dma((k - 1,)) for k in (ny, ny, ne, ne, ny, ny)]


def eliminate(tiles, t):
    n = tiles[0].shape[1]
    base = 8 * t
    lane = lax.broadcasted_iota(jnp.int32, (1, n), 1)
    lanes8 = lax.broadcasted_iota(jnp.int32, (8, n), 1)
    sub8 = lax.broadcasted_iota(jnp.int32, (8, n), 0)
    pivots = tiles[t]
    out = jnp.zeros((8, n), F32)
    columns = [jnp.broadcast_to(pivots[:, base + k:base + k + 1], (8, n)) for k in range(8)]
    for k in range(8):
        j = base + k
        pivot = columns[k][k:k + 1]
        scale = 1.0 / pivot
        row = jnp.where(lane == j, 1.0, pivots[k:k + 1])
        out = jnp.where(sub8 == k, jnp.where(lane <= j, row, 0.0) * lax.rsqrt(pivot), out)
        scaled = row * scale
        pivots = jnp.where(sub8 == k, scaled, jnp.where(lanes8 == j, 0.0, pivots) - columns[k] * scaled)
        for later in range(k + 1, 8):
            ratio = columns[later][k:k + 1] * scale
            columns[later] = jnp.where(sub8 == k, ratio, columns[later] - columns[k] * ratio)
    inside = (lanes8 >= base) & (lanes8 < base + 8)
    rest = list(tiles)
    for u in range(t + 1, n // 8):
        old = tiles[u]
        terms = [jnp.broadcast_to(old[:, base + k:base + k + 1], (8, n)) * pivots[k:k + 1] for k in range(8)]
        while len(terms) > 1:
            terms = [terms[i] + terms[i + 1] for i in range(0, len(terms), 2)]
        rest[u] = jnp.where(inside, 0.0, old) - terms[0]
    return out, rest


def reduce_kernel(sizes, cells, p_any, v_any, hi_ref, lo_ref, split_ref, stats_ref,
                  pext, vbuf, ylo, yhi, zlo, zhi, zsend, load_sem, hs, hr, *refs):
    nx, ny, nz = sizes
    ne = nx * nz
    cx, cy, cz, bands = p_any.shape
    first, second = Reduce(sizes, refs[:12]), Reduce(sizes, refs[12:])
    mx, my, mz = first.mx, first.my, first.mz

    load = pltpu.make_async_copy(p_any, pext.at[pl.ds(2, cx)], load_sem.at[0])
    load.start()
    load_v = pltpu.make_async_copy(v_any, vbuf, load_sem.at[1])
    load_v.start()
    barrier = pltpu.get_barrier_semaphore()
    for o in range(1, ny):
        pl.semaphore_signal(barrier, inc=1, device_id=first.line_peer(o), device_id_type=MESH)
    for o in range(1, ne):
        pl.semaphore_signal(barrier, inc=1, device_id=first.plane_peer(o), device_id_type=MESH)
    load.wait()
    own = pext[2:2 + cx]
    zsend[0] = own[:, :, cz - 2:, :]
    zsend[1] = own[:, :, :2, :]
    flat = own.reshape(cx * cy * cz, bands)
    rows = bands // ny

    def put(where, slot, matrix):
        for k in range(ny):
            where[k, slot * rows:(slot + 1) * rows] = matrix[k * rows:(k + 1) * rows]

    put(first.part, 0, gram(flat, flat))
    pl.semaphore_wait(barrier, ny - 1 + ne - 1)

    def remote(src, dst, i, device):
        return pltpu.make_async_remote_copy(src_ref=src, dst_ref=dst, send_sem=hs.at[i], recv_sem=hr.at[i],
                                            device_id=device, device_id_type=MESH)

    xf = (lax.rem(mx + 1, nx), my, mz)
    xb = (lax.rem(mx + nx - 1, nx), my, mz)
    yf = (mx, lax.rem(my + 1, ny), mz)
    yb = (mx, lax.rem(my + ny - 1, ny), mz)
    zf = (mx, my, lax.rem(mz + 1, nz))
    zb = (mx, my, lax.rem(mz + nz - 1, nz))
    halos = [
        remote(zsend.at[0], zlo, 0, zf),
        remote(zsend.at[1], zhi, 1, zb),
        remote(pext.at[pl.ds(cx, 2)], pext.at[pl.ds(0, 2)], 2, xf),
        remote(pext.at[pl.ds(2, 2)], pext.at[pl.ds(cx + 2, 2)], 3, xb),
        remote(pext.at[pl.ds(2, cx), pl.ds(cy - 2, 2)], ylo, 4, yf),
        remote(pext.at[pl.ds(2, cx), pl.ds(0, 2)], yhi, 5, yb),
    ]
    first.scatter()
    for copy in halos:
        copy.start()
    load_v.wait()
    first.exchange()
    for copy in halos:
        copy.wait()

    def plane(i, carry):
        center = pext[i + 2].astype(F32)
        one, two = 16.0 / -24.0, 1.0 / 24.0
        near = pext[i + 1].astype(F32) + pext[i + 3].astype(F32)
        far = pext[i].astype(F32) + pext[i + 4].astype(F32)
        ye = jnp.concatenate([ylo[i].astype(F32), center, yhi[i].astype(F32)], axis=0)
        near = near + (ye[1:1 + cy] + ye[3:3 + cy])
        far = far + (ye[0:cy] + ye[4:4 + cy])
        ze = jnp.concatenate([zlo[i].astype(F32), center, zhi[i].astype(F32)], axis=1)
        near = near + (ze[:, 1:1 + cz] + ze[:, 3:3 + cz])
        far = far + (ze[:, 0:cz] + ze[:, 4:4 + cz])
        level = vbuf[i][:, :, None] + 90.0 / 24.0
        applied = one * near + two * far + level * center
        hi, lo = split2(applied)
        hi_ref[i] = hi
        lo_ref[i] = lo
        return carry

    lax.fori_loop(0, cx, plane, 0)
    flat = pext[2:2 + cx].reshape(cx * cy * cz, bands)
    hi = hi_ref[...].reshape(cx * cy * cz, bands)
    lo = lo_ref[...].reshape(cx * cy * cz, bands)
    put(second.part, 0, gram(flat, hi) + gram(flat, lo))
    cross = gram(hi, lo)
    put(second.part, 1, gram(hi, hi) + cross + cross.T)
    second.scatter()
    first.gather()
    second.exchange()
    first.finish()

    correlation = first.gathered[...].reshape(bands, bands)
    matrix = correlation / cells
    count = bands // 8
    tiles = [matrix[8 * t:8 * t + 8] for t in range(count)]
    inverse = []
    for t in range(count):
        if t == count * 3 // 4:
            second.gather()
        out, tiles = eliminate(tiles, t)
        inverse.append(out)
    inverse_t = jnp.concatenate(inverse, axis=0).T
    for i, piece in enumerate(split3(inverse_t)):
        split_ref[:, i * bands:(i + 1) * bands] = piece
    second.finish()

    def quadratic(m):
        prod = jnp.dot(m, inverse_t, precision=lax.Precision.HIGHEST, preferred_element_type=F32)
        return jnp.sum(inverse_t * prod, axis=0, keepdims=True)

    rotated_all = quadratic(correlation)
    cross_all = quadratic(second.gathered[:, :rows].reshape(bands, bands))
    applied_all = quadratic(second.gathered[:, rows:].reshape(bands, bands))
    quotients = cross_all / cells
    squares = applied_all - 2.0 * quotients * cross_all + quotients * quotients * rotated_all
    stats_ref[0:1] = quotients
    stats_ref[1:2] = jnp.sqrt(squares / cells + 1e-06)


def dot(a, b):
    return jnp.dot(a, b, preferred_element_type=F32)


def finish_kernel(split_ref, stats_ref, p_ref, hi_ref, lo_ref, rot_ref, res_ref, quo_ref, norm_ref):
    bands = p_ref.shape[1]
    split = split_ref[...]
    p = p_ref[...]
    wide = dot(p, split[:, :2 * bands])
    rotated = wide[:, :bands] + (wide[:, bands:] + dot(p, split[:, 2 * bands:]))
    rot_ref[...] = rotated
    wide = dot(hi_ref[...], split[:, :2 * bands])
    applied = wide[:, :bands] + (wide[:, bands:] + dot(lo_ref[...], split[:, :bands]))
    res_ref[...] = (applied - stats_ref[0:1] * rotated).astype(BF16)
    quo_ref[...] = stats_ref[0:1]
    norm_ref[...] = stats_ref[1:2]


def local(sizes, wavefunctions, potential):
    nx, ny, nz = sizes
    cx, cy, cz, bands = wavefunctions.shape
    mine = cx * cy * cz
    vmem = pl.BlockSpec(memory_space=pltpu.VMEM)
    far = pl.BlockSpec(memory_space=pltpu.HBM)
    dma = pltpu.SemaphoreType.DMA
    hi, lo, split, stats = pl.pallas_call(
        functools.partial(reduce_kernel, sizes, float(mine * nx * ny * nz)),
        out_shape=(
            jax.ShapeDtypeStruct(wavefunctions.shape, BF16),
            jax.ShapeDtypeStruct(wavefunctions.shape, BF16),
            jax.ShapeDtypeStruct((bands, 3 * bands), BF16),
            jax.ShapeDtypeStruct((8, bands), F32),
        ),
        in_specs=[far, far],
        out_specs=(vmem, vmem, vmem, vmem),
        scratch_shapes=[
            pltpu.VMEM((cx + 4, cy, cz, bands), BF16),
            pltpu.VMEM((cx, cy, cz), F32),
            pltpu.VMEM((cx, 2, cz, bands), BF16),
            pltpu.VMEM((cx, 2, cz, bands), BF16),
            pltpu.VMEM((cx, cy, 2, bands), BF16),
            pltpu.VMEM((cx, cy, 2, bands), BF16),
            pltpu.VMEM((2, cx, cy, 2, bands), BF16),
            dma((2,)), dma((6,)), dma((6,)),
            *reduce_scratch(sizes, bands, bands),
            *reduce_scratch(sizes, 2 * bands, bands),
        ],
        compiler_params=pltpu.CompilerParams(collective_id=0, has_side_effects=True, vmem_limit_bytes=48 * 1024 * 1024),
    )(wavefunctions, potential)
    steps = 8 if mine % 128 == 0 else 1
    tile = mine // steps
    block = pl.BlockSpec((tile, bands), lambda i: (i, 0))
    line = pl.BlockSpec((1, bands), lambda i: (0, 0))
    rotated, residual, quotients, norms = pl.pallas_call(
        finish_kernel,
        grid=(steps,),
        out_shape=(
            jax.ShapeDtypeStruct((mine, bands), F32),
            jax.ShapeDtypeStruct((mine, bands), BF16),
            jax.ShapeDtypeStruct((1, bands), F32),
            jax.ShapeDtypeStruct((1, bands), F32),
        ),
        in_specs=[pl.BlockSpec((bands, 3 * bands), lambda i: (0, 0)), pl.BlockSpec((8, bands), lambda i: (0, 0)),
                  block, block, block],
        out_specs=(block, block, line, line),
        compiler_params=pltpu.CompilerParams(vmem_limit_bytes=48 * 1024 * 1024),
    )(split, stats, wavefunctions.reshape(mine, bands), hi.reshape(mine, bands), lo.reshape(mine, bands))
    shape = wavefunctions.shape
    return rotated.reshape(shape), residual.reshape(shape), quotients.reshape(bands), norms.reshape(bands)


def solution(mesh):
    sizes = (mesh.shape["gx"], mesh.shape["gy"], mesh.shape["gz"])
    placed = (P("gx", "gy", "gz", None), P("gx", "gy", "gz"))
    return jax.shard_map(
        functools.partial(local, sizes),
        mesh=mesh,
        in_specs=placed,
        out_specs=(P("gx", "gy", "gz", None), P("gx", "gy", "gz", None), P(), P()),
        check_vma=False,
    )
```

```python
import functools

import jax
import jax.numpy as jnp
from jax import lax
from jax.experimental import pallas as pl
from jax.experimental.pallas import tpu as pltpu
from jax.sharding import PartitionSpec as P

MESH = pl.DeviceIdType.MESH
F32 = jnp.float32
BF16 = jnp.bfloat16


def split2(a):
    hi = a.astype(BF16)
    return hi, (a - hi.astype(F32)).astype(BF16)


def split3(a):
    hi = a.astype(BF16)
    rest = a - hi.astype(F32)
    mid = rest.astype(BF16)
    return hi, mid, (rest - mid.astype(F32)).astype(BF16)


def gram(a, b):
    return lax.dot_general(a, b, (((0,), (0,)), ((), ())), preferred_element_type=F32)


class Reduce:
    def __init__(self, sizes, refs):
        self.part, self.got1, self.acc, self.got2, self.total, self.gathered = refs[:6]
        self.s1, self.r1, self.s2, self.r2, self.s3, self.r3 = refs[6:]
        self.nx, self.ny, self.nz = sizes
        self.ne = self.nx * self.nz
        self.mx, self.my, self.mz = lax.axis_index("gx"), lax.axis_index("gy"), lax.axis_index("gz")
        self.me = self.mx * self.nz + self.mz

    def line_peer(self, offset):
        return (self.mx, lax.rem(self.my + offset, self.ny), self.mz)

    def plane_peer(self, offset):
        e = lax.rem(self.me + offset, self.ne)
        return (e // self.nz, self.my, lax.rem(e, self.nz))

    def scatter_copy(self, o):
        return pltpu.make_async_remote_copy(
            src_ref=self.part.at[lax.rem(self.my + o, self.ny)], dst_ref=self.got1.at[o - 1],
            send_sem=self.s1.at[o - 1], recv_sem=self.r1.at[o - 1],
            device_id=self.line_peer(o), device_id_type=MESH)

    def exchange_copy(self, o, slot):
        return pltpu.make_async_remote_copy(
            src_ref=self.acc, dst_ref=self.got2.at[slot], send_sem=self.s2.at[o - 1], recv_sem=self.r2.at[o - 1],
            device_id=self.plane_peer(o), device_id_type=MESH)

    def gather_copy(self, o, slot):
        return pltpu.make_async_remote_copy(
            src_ref=self.total, dst_ref=self.gathered.at[slot], send_sem=self.s3.at[o - 1], recv_sem=self.r3.at[o - 1],
            device_id=self.line_peer(o), device_id_type=MESH)

    def scatter(self):
        for o in range(1, self.ny):
            self.scatter_copy(o).start()

    def exchange(self):
        for o in range(1, self.ny):
            self.scatter_copy(o).wait()
        mine = self.part[self.my]
        for o in range(1, self.ny):
            mine = mine + self.got1[o - 1]
        self.acc[...] = mine
        for o in range(1, self.ne):
            self.exchange_copy(o, self.me).start()
        self.got2[self.me] = mine

    def gather(self):
        for o in range(1, self.ne):
            self.exchange_copy(o, self.me).wait_send()
            self.exchange_copy(o, lax.rem(self.me + self.ne - o, self.ne)).wait_recv()
        whole = self.got2[0]
        for e in range(1, self.ne):
            whole = whole + self.got2[e]
        self.total[...] = whole
        for o in range(1, self.ny):
            self.gather_copy(o, self.my).start()
        self.gathered[self.my] = whole

    def finish(self):
        for o in range(1, self.ny):
            self.gather_copy(o, self.my).wait_send()
            self.gather_copy(o, lax.rem(self.my + self.ny - o, self.ny)).wait_recv()


def reduce_scratch(sizes, chunk, bands):
    nx, ny, nz = sizes
    ne = nx * nz
    dma = pltpu.SemaphoreType.DMA
    shapes = ((ny, chunk), (ny - 1, chunk), (chunk,), (ne, chunk), (chunk,), (ny, chunk))
    return [pltpu.VMEM(shape + (bands,), F32) for shape in shapes] + [dma((k - 1,)) for k in (ny, ny, ne, ne, ny, ny)]


def eliminate(tiles, t):
    n = tiles[0].shape[1]
    base = 8 * t
    lane = lax.broadcasted_iota(jnp.int32, (1, n), 1)
    lanes8 = lax.broadcasted_iota(jnp.int32, (8, n), 1)
    sub8 = lax.broadcasted_iota(jnp.int32, (8, n), 0)
    pivots = tiles[t]
    out = jnp.zeros((8, n), F32)
    columns = [jnp.broadcast_to(pivots[:, base + k:base + k + 1], (8, n)) for k in range(8)]
    for k in range(8):
        j = base + k
        pivot = columns[k][k:k + 1]
        scale = 1.0 / pivot
        row = jnp.where(lane == j, 1.0, pivots[k:k + 1])
        out = jnp.where(sub8 == k, jnp.where(lane <= j, row, 0.0) * lax.rsqrt(pivot), out)
        scaled = row * scale
        pivots = jnp.where(sub8 == k, scaled, jnp.where(lanes8 == j, 0.0, pivots) - columns[k] * scaled)
        for later in range(k + 1, 8):
            ratio = columns[later][k:k + 1] * scale
            columns[later] = jnp.where(sub8 == k, ratio, columns[later] - columns[k] * ratio)
    inside = (lanes8 >= base) & (lanes8 < base + 8)
    rest = list(tiles)
    for u in range(t + 1, n // 8):
        old = tiles[u]
        terms = [jnp.broadcast_to(old[:, base + k:base + k + 1], (8, n)) * pivots[k:k + 1] for k in range(8)]
        while len(terms) > 1:
            terms = [terms[i] + terms[i + 1] for i in range(0, len(terms), 2)]
        rest[u] = jnp.where(inside, 0.0, old) - terms[0]
    return out, rest


def reduce_kernel(sizes, cells, p_any, v_any, rot_ref, app_ref, stats_ref,
                  hi_ref, lo_ref, split_ref, pext, vbuf, ylo, yhi, zlo, zhi, zsend, load_sem, hs, hr, *refs):
    nx, ny, nz = sizes
    ne = nx * nz
    cx, cy, cz, bands = p_any.shape
    first, second = Reduce(sizes, refs[:12]), Reduce(sizes, refs[12:])
    mx, my, mz = first.mx, first.my, first.mz

    load = pltpu.make_async_copy(p_any, pext.at[pl.ds(2, cx)], load_sem.at[0])
    load.start()
    load_v = pltpu.make_async_copy(v_any, vbuf, load_sem.at[1])
    load_v.start()
    barrier = pltpu.get_barrier_semaphore()
    for o in range(1, ny):
        pl.semaphore_signal(barrier, inc=1, device_id=first.line_peer(o), device_id_type=MESH)
    for o in range(1, ne):
        pl.semaphore_signal(barrier, inc=1, device_id=first.plane_peer(o), device_id_type=MESH)
    load.wait()
    pl.semaphore_wait(barrier, ny - 1 + ne - 1)

    def remote(src, dst, i, device):
        return pltpu.make_async_remote_copy(src_ref=src, dst_ref=dst, send_sem=hs.at[i], recv_sem=hr.at[i],
                                            device_id=device, device_id_type=MESH)

    xf = (lax.rem(mx + 1, nx), my, mz)
    xb = (lax.rem(mx + nx - 1, nx), my, mz)
    yf = (mx, lax.rem(my + 1, ny), mz)
    yb = (mx, lax.rem(my + ny - 1, ny), mz)
    zf = (mx, my, lax.rem(mz + 1, nz))
    zb = (mx, my, lax.rem(mz + nz - 1, nz))
    outer = [
        remote(pext.at[pl.ds(cx, 2)], pext.at[pl.ds(0, 2)], 2, xf),
        remote(pext.at[pl.ds(2, 2)], pext.at[pl.ds(cx + 2, 2)], 3, xb),
    ]
    inner = [
        remote(pext.at[pl.ds(2, cx), pl.ds(cy - 2, 2)], ylo, 4, yf),
        remote(pext.at[pl.ds(2, cx), pl.ds(0, 2)], yhi, 5, yb),
        remote(zsend.at[0], zlo, 0, zf),
        remote(zsend.at[1], zhi, 1, zb),
    ]
    for copy in inner[:2] + outer:
        copy.start()
    own = pext[2:2 + cx]
    zsend[0] = own[:, :, cz - 2:, :]
    zsend[1] = own[:, :, :2, :]
    for copy in inner[2:]:
        copy.start()
    rows = bands // ny

    def cells_of(ref, start, stop):
        return ref[start:stop].reshape((stop - start) * cy * cz, bands)

    flat = cells_of(pext, 2, 2 + cx)
    matrix = gram(flat, flat)
    for k in range(ny):
        first.part[k] = matrix[k * rows:(k + 1) * rows]
    first.scatter()
    load_v.wait()
    for copy in inner:
        copy.wait()

    def plane(i, carry):
        center = pext[i + 2].astype(F32)
        one, two = 16.0 / -24.0, 1.0 / 24.0
        near = pext[i + 1].astype(F32) + pext[i + 3].astype(F32)
        far = pext[i].astype(F32) + pext[i + 4].astype(F32)
        ye = jnp.concatenate([ylo[i].astype(F32), center, yhi[i].astype(F32)], axis=0)
        near = near + (ye[1:1 + cy] + ye[3:3 + cy])
        far = far + (ye[0:cy] + ye[4:4 + cy])
        ze = jnp.concatenate([zlo[i].astype(F32), center, zhi[i].astype(F32)], axis=1)
        near = near + (ze[:, 1:1 + cz] + ze[:, 3:3 + cz])
        far = far + (ze[:, 0:cz] + ze[:, 4:4 + cz])
        level = vbuf[i][:, :, None] + 90.0 / 24.0
        applied = one * near + two * far + level * center
        hi, lo = split2(applied)
        hi_ref[i] = hi
        lo_ref[i] = lo
        return carry

    lax.fori_loop(2, cx - 2, plane, 0)
    first.exchange()

    def grams(start, stop):
        p = cells_of(pext, 2 + start, 2 + stop)
        hi, lo = cells_of(hi_ref, start, stop), cells_of(lo_ref, start, stop)
        return gram(p, hi) + gram(p, lo), gram(hi, hi), gram(hi, lo)

    most = grams(2, cx - 2)
    for copy in outer:
        copy.wait()
    for i in (0, 1, cx - 2, cx - 1):
        plane(i, 0)
    cross, square, mixed = [a + b + c for a, b, c in zip(most, grams(0, 2), grams(cx - 2, cx))]
    square = square + mixed + mixed.T
    row = lax.broadcasted_iota(jnp.int32, (bands, bands), 0)
    col = lax.broadcasted_iota(jnp.int32, (bands, bands), 1)
    diagonal = jnp.sum(jnp.where(row == col, cross, 0.0), axis=0, keepdims=True)
    packed = jnp.where(row < col, cross + cross.T, jnp.where(row > col, 2.0 * square, square))
    for k in range(ny):
        second.part[k, :rows] = packed[k * rows:(k + 1) * rows]
        second.part[k, rows:] = jnp.broadcast_to(diagonal, (8, bands))
    second.scatter()
    first.gather()
    second.exchange()
    first.finish()

    correlation = first.gathered[...].reshape(bands, bands)
    matrix = correlation / cells
    count = bands // 8
    tiles = [matrix[8 * t:8 * t + 8] for t in range(count)]
    inverse = []
    for t in range(count):
        out, tiles = eliminate(tiles, t)
        inverse.append(out)
    inverse_t = jnp.concatenate(inverse, axis=0).T
    for i, piece in enumerate(split3(inverse_t)):
        split_ref[:, i * bands:(i + 1) * bands] = piece
    second.gather()
    planes = 4 if cx % 4 == 0 else 1

    def rotate(i, carry):
        at = pl.ds(i * planes, planes)
        shape = (planes * cy * cz, bands)
        split = split_ref[...]
        p = pext[pl.ds(i * planes + 2, planes)].reshape(shape)
        wide = dot(p, split[:, :2 * bands])
        rot_ref[at] = (wide[:, :bands] + (wide[:, bands:] + dot(p, split[:, 2 * bands:]))).reshape(planes, cy, cz, bands)
        wide = dot(hi_ref[at].reshape(shape), split[:, :2 * bands])
        applied = wide[:, :bands] + (wide[:, bands:] + dot(lo_ref[at].reshape(shape), split[:, :bands]))
        app_ref[at] = applied.reshape(planes, cy, cz, bands)
        return carry

    lax.fori_loop(0, cx // planes, rotate, 0)
    second.finish()

    def quadratic(m):
        prod = jnp.dot(m, inverse_t, precision=lax.Precision.HIGHEST, preferred_element_type=F32)
        return jnp.sum(inverse_t * prod, axis=0, keepdims=True)

    rotated_all = quadratic(correlation)
    sums = second.gathered[:, :rows].reshape(bands, bands)
    diagonal = second.gathered[0, rows:rows + 1]
    cross_all = quadratic(jnp.where(row < col, sums, jnp.where(row == col, diagonal, 0.0)))
    applied_all = quadratic(jnp.where(row < col, 0.0, sums))
    quotients = cross_all / cells
    squares = applied_all - 2.0 * quotients * cross_all + quotients * quotients * rotated_all
    stats_ref[0:1] = quotients
    stats_ref[1:2] = jnp.sqrt(squares / cells + 1e-06)


def dot(a, b):
    return jnp.dot(a, b, preferred_element_type=F32)


def finish_kernel(stats_ref, given_ref, app_ref, rot_ref, res_ref, quo_ref, norm_ref):
    rotated = given_ref[...]
    rot_ref[...] = rotated
    res_ref[...] = (app_ref[...] - stats_ref[0:1] * rotated).astype(BF16)
    quo_ref[...] = stats_ref[0:1]
    norm_ref[...] = stats_ref[1:2]


def local(sizes, wavefunctions, potential):
    nx, ny, nz = sizes
    cx, cy, cz, bands = wavefunctions.shape
    mine = cx * cy * cz
    vmem = pl.BlockSpec(memory_space=pltpu.VMEM)
    far = pl.BlockSpec(memory_space=pltpu.HBM)
    dma = pltpu.SemaphoreType.DMA
    rotated, applied, stats = pl.pallas_call(
        functools.partial(reduce_kernel, sizes, float(mine * nx * ny * nz)),
        out_shape=(
            jax.ShapeDtypeStruct(wavefunctions.shape, F32),
            jax.ShapeDtypeStruct(wavefunctions.shape, F32),
            jax.ShapeDtypeStruct((8, bands), F32),
        ),
        in_specs=[far, far],
        out_specs=(vmem, vmem, vmem),
        scratch_shapes=[
            pltpu.VMEM(wavefunctions.shape, BF16),
            pltpu.VMEM(wavefunctions.shape, BF16),
            pltpu.VMEM((bands, 3 * bands), BF16),
            pltpu.VMEM((cx + 4, cy, cz, bands), BF16),
            pltpu.VMEM((cx, cy, cz), F32),
            pltpu.VMEM((cx, 2, cz, bands), BF16),
            pltpu.VMEM((cx, 2, cz, bands), BF16),
            pltpu.VMEM((cx, cy, 2, bands), BF16),
            pltpu.VMEM((cx, cy, 2, bands), BF16),
            pltpu.VMEM((2, cx, cy, 2, bands), BF16),
            dma((2,)), dma((6,)), dma((6,)),
            *reduce_scratch(sizes, bands // ny, bands),
            *reduce_scratch(sizes, bands // ny + 8, bands),
        ],
        compiler_params=pltpu.CompilerParams(collective_id=0, has_side_effects=True, vmem_limit_bytes=48 * 1024 * 1024),
    )(wavefunctions, potential)
    steps = 8 if mine % 128 == 0 else 1
    tile = mine // steps
    block = pl.BlockSpec((tile, bands), lambda i: (i, 0))
    line = pl.BlockSpec((1, bands), lambda i: (0, 0))
    rotated, residual, quotients, norms = pl.pallas_call(
        finish_kernel,
        grid=(steps,),
        out_shape=(
            jax.ShapeDtypeStruct((mine, bands), F32),
            jax.ShapeDtypeStruct((mine, bands), BF16),
            jax.ShapeDtypeStruct((1, bands), F32),
            jax.ShapeDtypeStruct((1, bands), F32),
        ),
        in_specs=[pl.BlockSpec((8, bands), lambda i: (0, 0)), block, block],
        out_specs=(block, block, line, line),
        compiler_params=pltpu.CompilerParams(vmem_limit_bytes=48 * 1024 * 1024),
    )(stats, rotated.reshape(mine, bands), applied.reshape(mine, bands))
    shape = wavefunctions.shape
    return rotated.reshape(shape), residual.reshape(shape), quotients.reshape(bands), norms.reshape(bands)


def solution(mesh):
    sizes = (mesh.shape["gx"], mesh.shape["gy"], mesh.shape["gz"])
    placed = (P("gx", "gy", "gz", None), P("gx", "gy", "gz"))
    return jax.shard_map(
        functools.partial(local, sizes),
        mesh=mesh,
        in_specs=placed,
        out_specs=(P("gx", "gy", "gz", None), P("gx", "gy", "gz", None), P(), P()),
        check_vma=False,
    )
```

```python
import functools

import jax
import jax.numpy as jnp
from jax import lax
from jax.experimental import pallas as pl
from jax.experimental.pallas import tpu as pltpu
from jax.sharding import PartitionSpec as P

MESH = pl.DeviceIdType.MESH
F32 = jnp.float32
BF16 = jnp.bfloat16


def split2(a):
    hi = a.astype(BF16)
    return hi, (a - hi.astype(F32)).astype(BF16)


def split3(a):
    hi = a.astype(BF16)
    rest = a - hi.astype(F32)
    mid = rest.astype(BF16)
    return hi, mid, (rest - mid.astype(F32)).astype(BF16)


def gram(a, b):
    return lax.dot_general(a, b, (((0,), (0,)), ((), ())), preferred_element_type=F32)


class Reduce:
    def __init__(self, sizes, refs):
        self.part, self.got1, self.acc, self.got2, self.total, self.gathered = refs[:6]
        self.s1, self.r1, self.s2, self.r2, self.s3, self.r3 = refs[6:]
        self.nx, self.ny, self.nz = sizes
        self.ne = self.nx * self.nz
        self.mx, self.my, self.mz = lax.axis_index("gx"), lax.axis_index("gy"), lax.axis_index("gz")
        self.me = self.mx * self.nz + self.mz

    def line_peer(self, offset):
        return (self.mx, lax.rem(self.my + offset, self.ny), self.mz)

    def plane_peer(self, offset):
        e = lax.rem(self.me + offset, self.ne)
        return (e // self.nz, self.my, lax.rem(e, self.nz))

    def scatter_copy(self, o):
        return pltpu.make_async_remote_copy(
            src_ref=self.part.at[lax.rem(self.my + o, self.ny)], dst_ref=self.got1.at[o - 1],
            send_sem=self.s1.at[o - 1], recv_sem=self.r1.at[o - 1],
            device_id=self.line_peer(o), device_id_type=MESH)

    def exchange_copy(self, o, slot):
        return pltpu.make_async_remote_copy(
            src_ref=self.acc, dst_ref=self.got2.at[slot], send_sem=self.s2.at[o - 1], recv_sem=self.r2.at[o - 1],
            device_id=self.plane_peer(o), device_id_type=MESH)

    def gather_copy(self, o, slot):
        return pltpu.make_async_remote_copy(
            src_ref=self.total, dst_ref=self.gathered.at[slot], send_sem=self.s3.at[o - 1], recv_sem=self.r3.at[o - 1],
            device_id=self.line_peer(o), device_id_type=MESH)

    def scatter(self):
        for o in range(1, self.ny):
            self.scatter_copy(o).start()

    def exchange(self):
        for o in range(1, self.ny):
            self.scatter_copy(o).wait()
        mine = self.part[self.my]
        for o in range(1, self.ny):
            mine = mine + self.got1[o - 1]
        self.acc[...] = mine
        for o in range(1, self.ne):
            self.exchange_copy(o, self.me).start()
        self.got2[self.me] = mine

    def gather(self):
        for o in range(1, self.ne):
            self.exchange_copy(o, self.me).wait_send()
            self.exchange_copy(o, lax.rem(self.me + self.ne - o, self.ne)).wait_recv()
        whole = self.got2[0]
        for e in range(1, self.ne):
            whole = whole + self.got2[e]
        self.total[...] = whole
        for o in range(1, self.ny):
            self.gather_copy(o, self.my).start()
        self.gathered[self.my] = whole

    def finish(self):
        for o in range(1, self.ny):
            self.gather_copy(o, self.my).wait_send()
            self.gather_copy(o, lax.rem(self.my + self.ny - o, self.ny)).wait_recv()


def reduce_scratch(sizes, chunk, bands):
    nx, ny, nz = sizes
    ne = nx * nz
    dma = pltpu.SemaphoreType.DMA
    shapes = ((ny, chunk), (ny - 1, chunk), (chunk,), (ne, chunk), (chunk,), (ny, chunk))
    return [pltpu.VMEM(shape + (bands,), F32) for shape in shapes] + [dma((k - 1,)) for k in (ny, ny, ne, ne, ny, ny)]


def eliminate(tiles, t):
    n = tiles[0].shape[1]
    base = 8 * t
    lane = lax.broadcasted_iota(jnp.int32, (1, n), 1)
    lanes8 = lax.broadcasted_iota(jnp.int32, (8, n), 1)
    sub8 = lax.broadcasted_iota(jnp.int32, (8, n), 0)
    pivots = tiles[t]
    out = jnp.zeros((8, n), F32)
    columns = [jnp.broadcast_to(pivots[:, base + k:base + k + 1], (8, n)) for k in range(8)]
    for k in range(8):
        j = base + k
        pivot = columns[k][k:k + 1]
        scale = 1.0 / pivot
        row = jnp.where(lane == j, 1.0, pivots[k:k + 1])
        out = jnp.where(sub8 == k, jnp.where(lane <= j, row, 0.0) * lax.rsqrt(pivot), out)
        scaled = row * scale
        pivots = jnp.where(sub8 == k, scaled, jnp.where(lanes8 == j, 0.0, pivots) - columns[k] * scaled)
        for later in range(k + 1, 8):
            ratio = columns[later][k:k + 1] * scale
            columns[later] = jnp.where(sub8 == k, ratio, columns[later] - columns[k] * ratio)
    inside = (lanes8 >= base) & (lanes8 < base + 8)
    rest = list(tiles)
    for u in range(t + 1, n // 8):
        old = tiles[u]
        terms = [jnp.broadcast_to(old[:, base + k:base + k + 1], (8, n)) * pivots[k:k + 1] for k in range(8)]
        while len(terms) > 1:
            terms = [terms[i] + terms[i + 1] for i in range(0, len(terms), 2)]
        rest[u] = jnp.where(inside, 0.0, old) - terms[0]
    return out, rest


def reduce_kernel(sizes, cells, p_any, v_any, rot_ref, app_ref, stats_ref,
                  hi_ref, lo_ref, split_ref, pext, vbuf, ylo, yhi, zlo, zhi, zsend, load_sem, hs, hr, *refs):
    nx, ny, nz = sizes
    ne = nx * nz
    cx, cy, cz, bands = p_any.shape
    first, second = Reduce(sizes, refs[:12]), Reduce(sizes, refs[12:])
    mx, my, mz = first.mx, first.my, first.mz

    load = pltpu.make_async_copy(p_any, pext.at[pl.ds(2, cx)], load_sem.at[0])
    load.start()
    load_v = pltpu.make_async_copy(v_any, vbuf, load_sem.at[1])
    load_v.start()
    barrier = pltpu.get_barrier_semaphore()
    for o in range(1, ny):
        pl.semaphore_signal(barrier, inc=1, device_id=first.line_peer(o), device_id_type=MESH)
    for o in range(1, ne):
        pl.semaphore_signal(barrier, inc=1, device_id=first.plane_peer(o), device_id_type=MESH)
    load.wait()
    pl.semaphore_wait(barrier, ny - 1 + ne - 1)

    def remote(src, dst, i, device):
        return pltpu.make_async_remote_copy(src_ref=src, dst_ref=dst, send_sem=hs.at[i], recv_sem=hr.at[i],
                                            device_id=device, device_id_type=MESH)

    xf = (lax.rem(mx + 1, nx), my, mz)
    xb = (lax.rem(mx + nx - 1, nx), my, mz)
    yf = (mx, lax.rem(my + 1, ny), mz)
    yb = (mx, lax.rem(my + ny - 1, ny), mz)
    zf = (mx, my, lax.rem(mz + 1, nz))
    zb = (mx, my, lax.rem(mz + nz - 1, nz))
    outer = [
        remote(pext.at[pl.ds(cx, 2)], pext.at[pl.ds(0, 2)], 2, xf),
        remote(pext.at[pl.ds(2, 2)], pext.at[pl.ds(cx + 2, 2)], 3, xb),
    ]
    inner = [
        remote(pext.at[pl.ds(2, cx), pl.ds(cy - 2, 2)], ylo, 4, yf),
        remote(pext.at[pl.ds(2, cx), pl.ds(0, 2)], yhi, 5, yb),
        remote(zsend.at[0], zlo, 0, zf),
        remote(zsend.at[1], zhi, 1, zb),
    ]
    for copy in inner[:2] + outer:
        copy.start()
    own = pext[2:2 + cx]
    zsend[0] = own[:, :, cz - 2:, :]
    zsend[1] = own[:, :, :2, :]
    for copy in inner[2:]:
        copy.start()
    rows = bands // ny

    def cells_of(ref, start, stop):
        return ref[start:stop].reshape((stop - start) * cy * cz, bands)

    flat = cells_of(pext, 2, 2 + cx)
    matrix = gram(flat, flat)
    for k in range(ny):
        first.part[k] = matrix[k * rows:(k + 1) * rows]
    first.scatter()
    load_v.wait()
    for copy in inner:
        copy.wait()

    def plane(i, carry):
        center = pext[i + 2].astype(F32)
        one, two = 16.0 / -24.0, 1.0 / 24.0
        near = pext[i + 1].astype(F32) + pext[i + 3].astype(F32)
        far = pext[i].astype(F32) + pext[i + 4].astype(F32)
        ye = jnp.concatenate([ylo[i].astype(F32), center, yhi[i].astype(F32)], axis=0)
        near = near + (ye[1:1 + cy] + ye[3:3 + cy])
        far = far + (ye[0:cy] + ye[4:4 + cy])
        ze = jnp.concatenate([zlo[i].astype(F32), center, zhi[i].astype(F32)], axis=1)
        near = near + (ze[:, 1:1 + cz] + ze[:, 3:3 + cz])
        far = far + (ze[:, 0:cz] + ze[:, 4:4 + cz])
        level = vbuf[i][:, :, None] + 90.0 / 24.0
        applied = one * near + two * far + level * center
        hi, lo = split2(applied)
        hi_ref[i] = hi
        lo_ref[i] = lo
        return carry

    lax.fori_loop(2, cx - 2, plane, 0)
    first.exchange()

    def grams(start, stop):
        p = cells_of(pext, 2 + start, 2 + stop)
        hi, lo = cells_of(hi_ref, start, stop), cells_of(lo_ref, start, stop)
        return gram(p, hi) + gram(p, lo), gram(hi, hi), gram(hi, lo)

    most = grams(2, cx - 2)
    for copy in outer:
        copy.wait()
    for i in (0, 1, cx - 2, cx - 1):
        plane(i, 0)
    cross, square, mixed = [a + b + c for a, b, c in zip(most, grams(0, 2), grams(cx - 2, cx))]
    square = square + mixed + mixed.T
    row = lax.broadcasted_iota(jnp.int32, (bands, bands), 0)
    col = lax.broadcasted_iota(jnp.int32, (bands, bands), 1)
    diagonal = jnp.sum(jnp.where(row == col, cross, 0.0), axis=0, keepdims=True)
    packed = jnp.where(row < col, cross + cross.T, jnp.where(row > col, 2.0 * square, square))
    for k in range(ny):
        second.part[k, :rows] = packed[k * rows:(k + 1) * rows]
        second.part[k, rows:] = jnp.broadcast_to(diagonal, (8, bands))
    second.scatter()
    first.gather()
    second.exchange()
    first.finish()

    correlation = first.gathered[...].reshape(bands, bands)
    matrix = correlation / cells
    count = bands // 8
    tiles = [matrix[8 * t:8 * t + 8] for t in range(count)]
    inverse = []
    for t in range(count):
        out, tiles = eliminate(tiles, t)
        inverse.append(out)
    inverse_t = jnp.concatenate(inverse, axis=0).T
    for i, piece in enumerate(split3(inverse_t)):
        split_ref[:, i * bands:(i + 1) * bands] = piece
    second.gather()
    planes = 4 if cx % 4 == 0 else 1

    def rotate(i, carry):
        at = pl.ds(i * planes, planes)
        shape = (planes * cy * cz, bands)
        split = split_ref[...]
        p = pext[pl.ds(i * planes + 2, planes)].reshape(shape)
        wide = dot(p, split[:, :2 * bands])
        rot_ref[at] = (wide[:, :bands] + (wide[:, bands:] + dot(p, split[:, 2 * bands:]))).reshape(planes, cy, cz, bands)
        wide = dot(hi_ref[at].reshape(shape), split[:, :2 * bands])
        applied = wide[:, :bands] + (wide[:, bands:] + dot(lo_ref[at].reshape(shape), split[:, :bands]))
        app_ref[at] = applied.reshape(planes, cy, cz, bands)
        return carry

    lax.fori_loop(0, cx // planes, rotate, 0)
    second.finish()

    def quadratic(m):
        prod = jnp.dot(m, inverse_t, precision=lax.Precision.HIGHEST, preferred_element_type=F32)
        return jnp.sum(inverse_t * prod, axis=0, keepdims=True)

    rotated_all = quadratic(correlation)
    sums = second.gathered[:, :rows].reshape(bands, bands)
    diagonal = second.gathered[0, rows:rows + 1]
    cross_all = quadratic(jnp.where(row < col, sums, jnp.where(row == col, diagonal, 0.0)))
    applied_all = quadratic(jnp.where(row < col, 0.0, sums))
    quotients = cross_all / cells
    squares = applied_all - 2.0 * quotients * cross_all + quotients * quotients * rotated_all
    stats_ref[0:1] = quotients
    stats_ref[1:2] = jnp.sqrt(squares / cells + 1e-06)


def dot(a, b):
    return jnp.dot(a, b, preferred_element_type=F32)


def finish_kernel(stats_ref, given_ref, app_ref, rot_ref, res_ref, quo_ref, norm_ref):
    rotated = given_ref[...]
    rot_ref[...] = rotated
    res_ref[...] = (app_ref[...] - stats_ref[0:1] * rotated).astype(BF16)
    quo_ref[...] = stats_ref[0:1]
    norm_ref[...] = stats_ref[1:2]


def local(sizes, wavefunctions, potential):
    nx, ny, nz = sizes
    cx, cy, cz, bands = wavefunctions.shape
    mine = cx * cy * cz
    vmem = pl.BlockSpec(memory_space=pltpu.VMEM)
    far = pl.BlockSpec(memory_space=pltpu.HBM)
    dma = pltpu.SemaphoreType.DMA
    rotated, applied, stats = pl.pallas_call(
        functools.partial(reduce_kernel, sizes, float(mine * nx * ny * nz)),
        out_shape=(
            jax.ShapeDtypeStruct(wavefunctions.shape, F32),
            jax.ShapeDtypeStruct(wavefunctions.shape, F32),
            jax.ShapeDtypeStruct((8, bands), F32),
        ),
        in_specs=[far, far],
        out_specs=(vmem, vmem, vmem),
        scratch_shapes=[
            pltpu.VMEM(wavefunctions.shape, BF16),
            pltpu.VMEM(wavefunctions.shape, BF16),
            pltpu.VMEM((bands, 3 * bands), BF16),
            pltpu.VMEM((cx + 4, cy, cz, bands), BF16),
            pltpu.VMEM((cx, cy, cz), F32),
            pltpu.VMEM((cx, 2, cz, bands), BF16),
            pltpu.VMEM((cx, 2, cz, bands), BF16),
            pltpu.VMEM((cx, cy, 2, bands), BF16),
            pltpu.VMEM((cx, cy, 2, bands), BF16),
            pltpu.VMEM((2, cx, cy, 2, bands), BF16),
            dma((2,)), dma((6,)), dma((6,)),
            *reduce_scratch(sizes, bands // ny, bands),
            *reduce_scratch(sizes, bands // ny + 8, bands),
        ],
        compiler_params=pltpu.CompilerParams(collective_id=0, has_side_effects=True, vmem_limit_bytes=48 * 1024 * 1024),
    )(wavefunctions, potential)
    steps = 2 if mine % 128 == 0 else 1
    tile = mine // steps
    block = pl.BlockSpec((tile, bands), lambda i: (i, 0))
    line = pl.BlockSpec((1, bands), lambda i: (0, 0))
    rotated, residual, quotients, norms = pl.pallas_call(
        finish_kernel,
        grid=(steps,),
        out_shape=(
            jax.ShapeDtypeStruct((mine, bands), F32),
            jax.ShapeDtypeStruct((mine, bands), BF16),
            jax.ShapeDtypeStruct((1, bands), F32),
            jax.ShapeDtypeStruct((1, bands), F32),
        ),
        in_specs=[pl.BlockSpec((8, bands), lambda i: (0, 0)), block, block],
        out_specs=(block, block, line, line),
        compiler_params=pltpu.CompilerParams(vmem_limit_bytes=48 * 1024 * 1024),
    )(stats, rotated.reshape(mine, bands), applied.reshape(mine, bands))
    shape = wavefunctions.shape
    return rotated.reshape(shape), residual.reshape(shape), quotients.reshape(bands), norms.reshape(bands)


def solution(mesh):
    sizes = (mesh.shape["gx"], mesh.shape["gy"], mesh.shape["gz"])
    placed = (P("gx", "gy", "gz", None), P("gx", "gy", "gz"))
    return jax.shard_map(
        functools.partial(local, sizes),
        mesh=mesh,
        in_specs=placed,
        out_specs=(P("gx", "gy", "gz", None), P("gx", "gy", "gz", None), P(), P()),
        check_vma=False,
    )
```
